32 devices in a mesh: seq: 16 (over z, x, core), head: 2 (over y).
Axes of the slice: x: 2, y: 2, z: 4, core: 2. Of those that a mesh axis runs over, the one named last changes fastest.
Arguments:
- features: bfloat16 [8, 32, 8, 512], P(None, 'seq', 'head'), may hold values from -540 to 540
- gn_gain: float32 [512], replicated, may hold values from 0.5 to 1.5
- gn_bias: float32 [512], replicated, may hold values from -3 to 3
- conv_weight: bfloat16 [3, 3, 3, 16, 512], replicated, may hold values from -0.0546875 to 0.0546875
- conv_bias: float32 [16], replicated, may hold values from -3 to 3
- patch_weight: bfloat16 [64, 3072], replicated, may hold values from -0.75 to 0.75
- patch_bias: float32 [3072], replicated, may hold values from -3 to 3
- image_mod: float32 [3, 3072], replicated, may hold values from -3 to 3
- w_qkv: bfloat16 [3072, 3, 2048], P('seq', None, 'head'), may hold values from -5 to 5
- text_ids: int32 [512], replicated, may hold values from 0 to 16383
- text_length: int32 [1], replicated, may hold values from 256 to 512
- text_table: bfloat16 [3072, 16384], P('seq'), may hold values from -60 to 60
- text_mod: float32 [2, 3072], P(None, 'seq'), may hold values from -3 to 3
- w_text: bfloat16 [3072, 2, 2048], P('seq', None, 'head'), may hold values from -2 to 2
- w_out: bfloat16 [2048, 3072], P('head'), may hold values from -0.625 to 0.625
- out_bias: float32 [3072], replicated, may hold values from -3 to 3
Outputs:
- block_out: bfloat16 [8, 16, 4, 3072], P(None, 'seq', 'head')
The draws below stay inside these ranges and needn't reach their ends.
All inputs are finite; a program needn't handle non-finite values.
Results may differ from the reference program's by a relative error of at most 0.0089.
Values may be sent and summed in bfloat16 or wider, within the bound.
A program may use at most 128 MiB of HBM per device.

```python
import jax
import jax.numpy as jnp
from jax import lax

D = 3072
HEADS = 16
HD = 128
C_VAE = 512
GN_GROUPS = 32
ZC = 16
VOCAB = 16384
TXT = 512
FRAMES = 8
ROWS = 32
COLS = 8
TOKS = 512


def draw_features(key, part):
    base_key = jax.random.fold_in(key, 11)
    noise_key, chan_key = jax.random.split(base_key, 2)
    shape_all = (FRAMES, ROWS, COLS, C_VAE)
    noise_field = jnp.clip(jax.random.normal(noise_key, shape_all, jnp.float32), -6.0, 6.0)
    row_place = jnp.arange(ROWS, dtype=jnp.float32) / max(ROWS - 1, 1)
    row_scale = jnp.exp(jnp.log(3.0) * row_place)
    col_place = jnp.arange(COLS, dtype=jnp.float32) / max(COLS - 1, 1)
    col_scale = jnp.exp(jnp.log(3.0) * col_place)
    chan_scale = jnp.exp(jnp.log(10.0) * jax.random.uniform(chan_key, (C_VAE,), jnp.float32))
    return (noise_field * row_scale[None, :, None, None] * col_scale[None, None, :, None] * chan_scale).astype(jnp.bfloat16)


def draw_text_table(key, part):
    base_key = jax.random.fold_in(key, 23)
    noise_key, column_key = jax.random.split(base_key, 2)
    noise_field = jnp.clip(jax.random.normal(noise_key, (D, VOCAB), jnp.float32), -6.0, 6.0)
    feature_place = jnp.arange(D, dtype=jnp.float32) / (D - 1)
    feature_scale = jnp.exp(jnp.log(10.0) * feature_place)
    column_scale = jnp.exp(jnp.log(10.0) * jax.random.uniform(column_key, (VOCAB,), jnp.float32))
    return (0.1 * noise_field * feature_scale[:, None] * column_scale[None, :]).astype(jnp.bfloat16)


def draw_w_qkv(key, part):
    base_key = jax.random.fold_in(key, 37)
    noise_key, along_key, column_key, pick_key = jax.random.split(base_key, 4)
    shape_all = (D, 3, HEADS * HD)
    noise_field = 0.07 * jnp.clip(jax.random.normal(noise_key, shape_all, jnp.float32), -6.0, 6.0)
    strength = 7.0
    along = jnp.clip(jax.random.normal(along_key, (D,), jnp.float32), -4.0, 4.0) / D ** 0.5
    columns = jnp.clip(jax.random.normal(column_key, (HEADS, HD), jnp.float32), -3.0, 3.0)
    order = jax.random.permutation(pick_key, HEADS)
    level_list = jnp.array([0.45, 0.7, 1.0], jnp.float32)
    levels = jnp.zeros((HEADS,), jnp.float32).at[order[:3]].set(level_list)
    amplitude = (jnp.sqrt(strength * levels)[:, None] * columns).reshape(HEADS * HD)
    aligned = along[:, None] * amplitude[None, :]
    which_part = jnp.array([1.0, 1.0, 0.0], jnp.float32)
    return (noise_field + aligned[:, None, :] * which_part[None, :, None]).astype(jnp.bfloat16)


def plant(values, stream_key, low, high):
    extent = values.shape
    index_at = [jax.random.randint(jax.random.fold_in(stream_key, axis), (), 0, extent[axis]) for axis in range(len(extent))]
    values = values.at[tuple(index_at)].set(low)
    longest = extent.index(max(extent))
    index_at[longest] = (index_at[longest] + 1) % extent[longest]
    return values.at[tuple(index_at)].set(high)


def raised(drawn, rng, source, target, shards_of, factor):
    owner, partner = [(jnp.arange(drawn.shape[axis_at]) // (drawn.shape[axis_at] // shards_of)).reshape([-1 if axis == axis_at else 1 for axis in range(drawn.ndim)]) for axis_at in (source, target)]
    chosen = jax.random.permutation(rng, shards_of)[partner]
    strong = (owner == chosen) | (owner == (partner + shards_of // 2) % shards_of)
    return jnp.where(strong, factor * drawn, drawn)


def block_levels(own_key, extent, pieces, smallest, largest):
    loudness = 1.0
    for dim, parts in pieces:
        heights = jax.random.uniform(jax.random.fold_in(jax.random.fold_in(own_key, 6), dim), (parts,), jnp.float32, smallest / len(pieces), largest / len(pieces))
        loudness = loudness * jnp.repeat(jnp.exp(heights), extent[dim] // parts).reshape((-1,) + (1,) * (len(extent) - 1 - dim))
    return loudness


def scatter_about(key, dims, deviation, reach, pieces=(), kind=jnp.bfloat16):
    result = deviation * jax.random.normal(key, dims, jnp.float32)
    if pieces:
        result = result * block_levels(key, dims, pieces, -0.22, 0.18)
    return jnp.clip(result, -reach, reach).astype(kind)


def heavy_noise(key, dims, scale, bound, pieces, heavy, kind=jnp.bfloat16):
    result = scale * jax.random.normal(key, dims, jnp.float32)
    if pieces:
        result = result * block_levels(key, dims, pieces, -0.22, 0.18)
    return jnp.clip(raised(result, jax.random.fold_in(key, 3), *heavy), -bound, bound).astype(kind)


def setup_inputs(seed: int = 0) -> dict:
    key_of = jax.random.split(jax.random.key(seed), 17)
    features = draw_features(jax.random.fold_in(key_of[16], 71), 0)
    gn_gain = jnp.clip(1.0 + 0.1 * jax.random.normal(key_of[1], (C_VAE,), jnp.float32), 0.5, 1.5)
    gn_bias = scatter_about(key_of[2], (C_VAE,), 0.5, 3.0, (), jnp.float32)
    conv_weight = scatter_about(key_of[3], (3, 3, 3, ZC, C_VAE), (27 * C_VAE) ** -0.5, 0.0546875)
    conv_bias = scatter_about(key_of[4], (ZC,), 0.5, 3.0, (), jnp.float32)
    patch_weight = scatter_about(key_of[5], (4 * ZC, D), (4 * ZC) ** -0.5, 0.75)
    patch_bias = scatter_about(key_of[6], (D,), 0.5, 3.0, (), jnp.float32)
    image_mod = scatter_about(key_of[7], (3, D), 0.5, 3.0, (), jnp.float32)
    w_qkv = draw_w_qkv(jax.random.fold_in(key_of[16], 71), 0)
    text_ids = plant(jax.random.randint(key_of[9], (TXT,), 0, VOCAB), jax.random.fold_in(key_of[9], 1), 0, VOCAB - 1).astype(jnp.int32)
    text_length = jax.random.randint(key_of[10], (1,), TXT // 2, TXT + 1).astype(jnp.int32)
    text_table = draw_text_table(jax.random.fold_in(key_of[16], 71), 0)
    text_mod = scatter_about(key_of[12], (2, D), 0.5, 3.0, ((1, 16),), jnp.float32)
    w_text = heavy_noise(key_of[13], (D, 2, HEADS * HD), 0.1, 2.0, ((0, 16), (2, 2)), (0, 2, 16, 2.0))
    w_out = scatter_about(key_of[14], (HEADS * HD, D), (2.0 / (HEADS * HD) ** 0.5), 0.625, ((0, 2),))
    out_bias = scatter_about(key_of[15], (D,), 0.5, 3.0, (), jnp.float32)
    return {"features": features, "gn_gain": gn_gain, "gn_bias": gn_bias, "conv_weight": conv_weight, "conv_bias": conv_bias, "patch_weight": patch_weight, "patch_bias": patch_bias, "image_mod": image_mod, "w_qkv": w_qkv, "text_ids": text_ids, "text_length": text_length, "text_table": text_table, "text_mod": text_mod, "w_text": w_text, "w_out": w_out, "out_bias": out_bias}


eps_norm = 1e-06

def patchify(latent):
    frame_count, row_count, col_count, chan_count = latent.shape
    blocks = latent.reshape(frame_count, row_count // 2, 2, col_count // 2, 2, chan_count)
    blocks = blocks.transpose(0, 1, 3, 2, 4, 5)
    return blocks.reshape(frame_count * (row_count // 2) * (col_count // 2), 4 * chan_count)

def embed_tokens(patches, patch_weight, patch_bias, image_mod):
    hidden = jnp.dot(patches, patch_weight, preferred_element_type=jnp.float32) + patch_bias
    center = lax.optimization_barrier(jnp.mean(hidden, axis=1, keepdims=True))
    offset = hidden - center
    spread = lax.optimization_barrier(jnp.mean(offset * offset, axis=1, keepdims=True))
    normed = offset * lax.rsqrt(spread + eps_norm)
    modulated = (normed * (1.0 + image_mod[1]) + image_mod[0]).astype(jnp.bfloat16)
    return (hidden, modulated)

def reference(features, gn_gain, gn_bias, conv_weight, conv_bias, patch_weight, patch_bias, image_mod, w_qkv, text_ids, text_length, text_table, text_mod, w_text, w_out, out_bias):
    values = features.astype(jnp.float32)
    grouped = values.reshape(FRAMES, ROWS, COLS, GN_GROUPS, C_VAE // GN_GROUPS)
    cell_count = FRAMES * ROWS * COLS * (C_VAE // GN_GROUPS)
    group_mean = lax.optimization_barrier(jnp.sum(grouped, axis=(0, 1, 2, 4))) / cell_count
    group_square = lax.optimization_barrier(jnp.sum(grouped * grouped, axis=(0, 1, 2, 4))) / cell_count
    group_scale = lax.rsqrt(group_square - group_mean * group_mean + eps_norm)
    normed = ((grouped - group_mean[:, None]) * group_scale[:, None]).reshape(FRAMES, ROWS, COLS, C_VAE)
    activated = jax.nn.silu(normed * gn_gain + gn_bias).astype(jnp.bfloat16)
    padded = jnp.pad(activated, ((0, 0), (1, 1), (1, 1), (0, 0)))
    padded = jnp.concatenate([padded[:1], padded[:1], padded], axis=0)
    latent_sum = jnp.zeros((FRAMES, ROWS, COLS, ZC), jnp.float32)
    for time_off in range(3):
        for row_off in range(3):
            for col_off in range(3):
                window = padded[time_off:time_off + FRAMES, row_off:row_off + ROWS, col_off:col_off + COLS].astype(jnp.float32)
                kernel = conv_weight[time_off, row_off, col_off].astype(jnp.float32)
                latent_sum = latent_sum + jnp.einsum('fyxc,zc->fyxz', window, kernel)
    latent = (latent_sum + conv_bias).astype(jnp.bfloat16)
    hidden, modulated = embed_tokens(patchify(latent), patch_weight, patch_bias, image_mod)
    qkv = jnp.einsum('nd,dkj->nkj', modulated.astype(jnp.float32), w_qkv.astype(jnp.float32)).astype(jnp.bfloat16)
    context = jnp.take(text_table, text_ids, axis=1).astype(jnp.float32)
    text_mean = lax.optimization_barrier(jnp.sum(context, axis=0)) / D
    text_square = lax.optimization_barrier(jnp.sum(context * context, axis=0)) / D
    text_scale = lax.rsqrt(text_square - text_mean * text_mean + eps_norm)
    text_normed = (context - text_mean) * text_scale * (1.0 + text_mod[1][:, None]) + text_mod[0][:, None]
    text_kv = jnp.einsum('dt,dkj->tkj', text_normed, w_text.astype(jnp.float32), precision=lax.Precision.HIGHEST).astype(jnp.bfloat16)
    all_keys = jnp.concatenate([qkv[:, 1], text_kv[:, 0]], axis=0).reshape(TOKS + TXT, HEADS, HD).transpose(1, 0, 2)
    all_values = jnp.concatenate([qkv[:, 2], text_kv[:, 1]], axis=0).reshape(TOKS + TXT, HEADS, HD).transpose(1, 0, 2)
    queries = qkv[:, 0].reshape(TOKS, HEADS, HD).transpose(1, 0, 2)
    key_valid = jnp.arange(TOKS + TXT, dtype=jnp.int32) < TOKS + text_length[0]

    def one_head(operands):
        query_h, key_h, value_h = operands
        scores = jnp.dot(query_h, key_h.T, preferred_element_type=jnp.float32) / HD
        scores = jnp.where(key_valid[None, :], scores, -1e+30)
        row_top = lax.optimization_barrier(jnp.max(scores, axis=1, keepdims=True))
        probs = jnp.exp(scores - row_top)
        totals = lax.optimization_barrier(jnp.sum(probs, axis=1, keepdims=True))
        return jnp.dot(probs.astype(jnp.bfloat16), value_h, preferred_element_type=jnp.float32) / totals
    attended = lax.map(one_head, (queries, all_keys, all_values))
    attended = attended.transpose(1, 0, 2).reshape(TOKS, HEADS * HD).astype(jnp.bfloat16)
    projected = jnp.dot(attended, w_out, preferred_element_type=jnp.float32) + out_bias
    block_out = (hidden + image_mod[2] * projected).astype(jnp.bfloat16)
    return block_out.reshape(FRAMES, ROWS // 2, COLS // 2, D)
```

```python
import jax
import jax.numpy as jnp
from jax import lax
from jax.sharding import PartitionSpec as P

HD = 128
GN_GROUPS = 32
CHUNK = 512

eps_norm = 1e-06


def group_gather(piece, group, dim):
    if group == 1:
        return piece
    count = lax.axis_size("seq")
    if group == 2:
        other = lax.ppermute(piece, "seq", [(i, i ^ 1) for i in range(count)])
        first = lax.axis_index("seq") % 2 == 0
        return jnp.concatenate(
            [jnp.where(first, piece, other), jnp.where(first, other, piece)], axis=dim
        )
    members = [list(range(i, i + group)) for i in range(0, count, group)]
    return lax.all_gather(piece, "seq", axis=dim, tiled=True, axis_index_groups=members)


def group_norm(features, gn_gain, gn_bias):
    frame_count, row_count, col_count, chan_count = features.shape
    per_group = chan_count // GN_GROUPS
    values = features.astype(jnp.float32)
    chan_sums = jnp.stack(
        [jnp.sum(values, axis=(0, 1, 2)), jnp.sum(values * values, axis=(0, 1, 2))]
    )
    sums = jnp.sum(chan_sums.reshape(2, GN_GROUPS, per_group), axis=2)
    sums = lax.psum(sums, ("seq", "head"))
    cell_count = (
        frame_count * row_count * col_count * per_group * lax.axis_size("seq") * lax.axis_size("head")
    )
    mean = sums[0] / cell_count
    scale = lax.rsqrt(sums[1] / cell_count - mean * mean + eps_norm)
    mean = jnp.repeat(mean, per_group)
    scale = jnp.repeat(scale, per_group)
    normed = (values - mean) * scale
    return jax.nn.silu(normed * gn_gain + gn_bias).astype(jnp.bfloat16)


def join_rims(parts, block_dim, dim, unit):
    size = parts.shape[dim]
    blocks = parts.shape[block_dim]
    core = lax.slice_in_dim(parts, unit, size - unit, axis=dim)
    low = lax.slice_in_dim(parts, 0, unit, axis=dim)
    high = lax.slice_in_dim(parts, size - unit, size, axis=dim)
    low = lax.slice_in_dim(low, 1, blocks, axis=block_dim)
    high = lax.slice_in_dim(high, 0, blocks - 1, axis=block_dim)
    pad_low = [(0, 0)] * parts.ndim
    pad_low[block_dim] = (0, 1)
    pad_low[dim] = (size - 3 * unit, 0)
    pad_high = [(0, 0)] * parts.ndim
    pad_high[block_dim] = (1, 0)
    pad_high[dim] = (0, size - 3 * unit)
    return core + jnp.pad(low, pad_low) + jnp.pad(high, pad_high)


def all_patches(activated, conv_weight, conv_bias):
    seq_n, head_n = lax.axis_size("seq"), lax.axis_size("head")
    frame_count, row_count, col_count, _ = activated.shape
    chans = conv_weight.shape[3]
    padded = jnp.concatenate([activated[:1], activated[:1], activated], axis=0)
    shares = lax.conv_general_dilated(
        padded[None],
        conv_weight,
        (1, 1, 1),
        ((0, 0), (2, 2), (2, 2)),
        dimension_numbers=("NDHWC", "DHWOI", "NDHWC"),
        preferred_element_type=jnp.float32,
    )[0]
    flat = shares.reshape(-1, 128)
    parts = lax.all_gather(flat, ("seq", "head"), axis=0, tiled=False)
    parts = parts.reshape(
        seq_n, head_n, frame_count, row_count + 2, (col_count + 2) * chans
    )
    parts = join_rims(join_rims(parts, 0, 3, 1), 1, 4, chans)
    latent = (parts + jnp.tile(conv_bias, col_count)).astype(jnp.bfloat16)
    blocks = latent.reshape(
        seq_n, head_n, frame_count, row_count // 2, 2, col_count // 2, 2 * chans
    )
    blocks = blocks.transpose(0, 1, 2, 3, 5, 4, 6)
    own = frame_count * (row_count // 2) * (col_count // 2)
    return blocks.reshape(seq_n * head_n * own, 4 * chans)


def modulate(patches, patch_weight, patch_bias, image_mod):
    hidden = jnp.dot(patches, patch_weight, preferred_element_type=jnp.float32) + patch_bias
    center = jnp.mean(hidden, axis=1, keepdims=True)
    offset = hidden - center
    spread = jnp.mean(offset * offset, axis=1, keepdims=True)
    normed = offset * lax.rsqrt(spread + eps_norm)
    return (normed * (1.0 + image_mod[1]) + image_mod[0]).astype(jnp.bfloat16)


def body(
    features,
    gn_gain,
    gn_bias,
    conv_weight,
    conv_bias,
    patch_weight,
    patch_bias,
    image_mod,
    w_qkv,
    text_ids,
    text_length,
    text_table,
    text_mod,
    w_text,
    w_out,
    out_bias,
):
    frame_count, row_count, col_count, _ = features.shape
    width_full = patch_weight.shape[1]
    seq_n, head_n = lax.axis_size("seq"), lax.axis_size("head")
    seq_i, head_i = lax.axis_index("seq"), lax.axis_index("head")
    depth, _, head_width = w_qkv.shape
    heads_here = head_width // HD
    group = seq_n // heads_here
    cols = head_width // seq_n
    text_count = text_ids.shape[0]

    both = jnp.concatenate([w_qkv, w_text], axis=1).reshape(depth, 5, seq_n, cols)
    both = both.transpose(2, 0, 1, 3).reshape(seq_n, depth, 5 * cols)
    both = lax.all_to_all(both, "seq", split_axis=0, concat_axis=0, tiled=True)
    both = both.reshape(seq_n * depth, 5, cols)
    both = group_gather(both, group, 2)
    w_query, w_image, w_text_full = both[:, 0], both[:, 1:3], both[:, 3:5]

    chosen = (
        lax.broadcasted_iota(jnp.int32, (text_table.shape[1], text_count), 0) == text_ids[None, :]
    ).astype(jnp.bfloat16)
    own_context = jnp.dot(text_table, chosen, preferred_element_type=jnp.float32).astype(
        jnp.bfloat16
    )
    context = lax.all_gather(own_context, "seq", axis=0, tiled=True).astype(jnp.float32)
    mod = lax.all_gather(text_mod, "seq", axis=1, tiled=True)
    text_mean = jnp.sum(context, axis=0) / width_full
    text_square = jnp.sum(context * context, axis=0) / width_full
    text_scale = lax.rsqrt(text_square - text_mean * text_mean + eps_norm)
    text_normed = (context - text_mean) * text_scale * (1.0 + mod[1][:, None]) + mod[0][:, None]
    text_high = text_normed.astype(jnp.bfloat16)
    text_low = (text_normed - text_high.astype(jnp.float32)).astype(jnp.bfloat16)
    w_text_flat = w_text_full.reshape(width_full, 2 * HD)
    text_kv = sum(
        lax.dot_general(
            part, w_text_flat, (((0,), (0,)), ((), ())), preferred_element_type=jnp.float32
        )
        for part in (text_high, text_low)
    ).astype(jnp.bfloat16)

    activated = group_norm(features, gn_gain, gn_bias)
    patches = all_patches(activated, conv_weight, conv_bias)
    own = patches.shape[0] // (seq_n * head_n)
    part_rows = head_n * own // group
    my_part = seq_i % group
    chunk = min(CHUNK, patches.shape[0])

    def project(rows):
        modulated = modulate(rows, patch_weight, patch_bias, image_mod)
        kv = jnp.dot(
            modulated, w_image.reshape(width_full, 2 * HD), preferred_element_type=jnp.float32
        )
        query = jnp.dot(modulated, w_query, preferred_element_type=jnp.float32)
        query = lax.dynamic_index_in_dim(
            query.reshape(-1, group, part_rows, HD), my_part, axis=1, keepdims=False
        )
        return kv.astype(jnp.bfloat16), query.reshape(-1, HD).astype(jnp.bfloat16)

    if chunk == patches.shape[0]:
        image_kv, query = project(patches)
    else:
        image_kv, query = lax.map(project, patches.reshape(-1, chunk, patches.shape[1]))
        image_kv = image_kv.reshape(-1, 2 * HD)
        query = query.reshape(-1, HD)

    keys = jnp.concatenate([image_kv[:, :HD], text_kv[:, :HD]], axis=0)
    vals = jnp.concatenate([image_kv[:, HD:], text_kv[:, HD:]], axis=0)
    key_valid = (
        jnp.arange(keys.shape[0], dtype=jnp.int32) < image_kv.shape[0] + text_length[0]
    )
    scores = (
        lax.dot_general(query, keys, (((1,), (1,)), ((), ())), preferred_element_type=jnp.float32)
        / HD
    )
    scores = jnp.where(key_valid[None, :], scores, -1e30)
    probs = jnp.exp(scores - jnp.max(scores, axis=1, keepdims=True))
    totals = jnp.sum(probs, axis=1, keepdims=True)
    attended = (
        jnp.dot(probs.astype(jnp.bfloat16), vals, preferred_element_type=jnp.float32) / totals
    ).astype(jnp.bfloat16)

    attended = attended.reshape(seq_n, part_rows, HD)
    attended = lax.all_to_all(attended, "seq", split_axis=0, concat_axis=0, tiled=True)
    attended = attended.reshape(heads_here, group, part_rows, HD).transpose(1, 2, 0, 3)
    attended = attended.reshape(head_n * own, head_width)
    if head_n == 2:
        halves = attended.reshape(2, own, head_width)
        away = jnp.dot(
            lax.dynamic_index_in_dim(halves, 1 - head_i, 0, keepdims=False),
            w_out,
            preferred_element_type=jnp.float32,
        )
        here = jnp.dot(
            lax.dynamic_index_in_dim(halves, head_i, 0, keepdims=False),
            w_out,
            preferred_element_type=jnp.float32,
        )
        projected = here + lax.ppermute(away, "head", [(0, 1), (1, 0)]) + out_bias
    else:
        projected = (
            lax.psum_scatter(
                jnp.dot(attended, w_out, preferred_element_type=jnp.float32),
                "head",
                scatter_dimension=0,
                tiled=True,
            )
            + out_bias
        )
    own_patches = lax.dynamic_slice_in_dim(patches, (seq_i * head_n + head_i) * own, own, axis=0)
    hidden = jnp.dot(own_patches, patch_weight, preferred_element_type=jnp.float32) + patch_bias
    block_out = (hidden + image_mod[2] * projected).astype(jnp.bfloat16)
    return block_out.reshape(frame_count, row_count // 2, col_count // 2, width_full)


def solution(mesh):
    return jax.shard_map(
        body,
        mesh=mesh,
        in_specs=(
            P(None, "seq", "head", None),
            P(),
            P(),
            P(),
            P(),
            P(),
            P(),
            P(),
            P("seq", None, "head"),
            P(),
            P(),
            P("seq", None),
            P(None, "seq"),
            P("seq", None, "head"),
            P("head", None),
            P(),
        ),
        out_specs=P(None, "seq", "head", None),
        check_vma=False,
    )
```

```python
import functools

import jax
import jax.numpy as jnp
from jax import lax
from jax.experimental import pallas as pl
from jax.experimental.pallas import tpu as pltpu
from jax.sharding import PartitionSpec as P

HD = 128
GN_GROUPS = 32
CHUNK = 512

eps_norm = 1e-06


MESH = pl.DeviceIdType.MESH


def share_kernel(seq_n, head_n, x_ref, out_ref, local_sem, send_sem, recv_sem):
    count = seq_n * head_n
    me = lax.axis_index("seq") * head_n + lax.axis_index("head")

    def place(index):
        return (lax.div(index, head_n), lax.rem(index, head_n))

    barrier = pltpu.get_barrier_semaphore()

    def greet(off, carry):
        pl.semaphore_signal(
            barrier, inc=1, device_id=place(lax.rem(me + off, count)), device_id_type=MESH
        )
        return carry

    lax.fori_loop(1, count, greet, 0)
    pl.semaphore_wait(barrier, count - 1)

    def copy(off, slot):
        return pltpu.make_async_remote_copy(
            src_ref=x_ref,
            dst_ref=out_ref.at[slot],
            send_sem=send_sem.at[off],
            recv_sem=recv_sem.at[off],
            device_id=place(lax.rem(me + off, count)),
            device_id_type=MESH,
        )

    def send(off, carry):
        copy(off, me).start()
        return carry

    lax.fori_loop(1, count, send, 0)
    own = pltpu.make_async_copy(x_ref, out_ref.at[me], local_sem)
    own.start()
    own.wait()

    def finish(off, carry):
        copy(off, me).wait_send()
        copy(off, lax.rem(me + count - off, count)).wait_recv()
        return carry

    lax.fori_loop(1, count, finish, 0)


def share(x, collective_id):
    seq_n, head_n = lax.axis_size("seq"), lax.axis_size("head")
    count = seq_n * head_n
    return pl.pallas_call(
        functools.partial(share_kernel, seq_n, head_n),
        out_shape=jax.ShapeDtypeStruct((count, *x.shape), x.dtype),
        in_specs=[pl.BlockSpec(memory_space=pltpu.VMEM)],
        out_specs=pl.BlockSpec(memory_space=pltpu.VMEM),
        scratch_shapes=[
            pltpu.SemaphoreType.DMA,
            pltpu.SemaphoreType.DMA((count,)),
            pltpu.SemaphoreType.DMA((count,)),
        ],
        compiler_params=pltpu.CompilerParams(collective_id=collective_id, has_side_effects=True),
    )(x)


def weights_kernel(
    heads_here,
    group,
    wq_ref,
    wt_ref,
    ctx_ref,
    w_ref,
    full_ref,
    local_sem,
    send_sem,
    recv_sem,
    pass_send,
    pass_recv,
):
    s, h = lax.axis_index("seq"), lax.axis_index("head")
    mine, place = lax.div(s, group), lax.rem(s, group)
    width = heads_here * HD
    barrier = pltpu.get_barrier_semaphore()
    for off in range(1, heads_here):
        peer = lax.rem(mine + off, heads_here) * group + place
        pl.semaphore_signal(barrier, inc=1, device_id=(peer, h), device_id_type=MESH)
    for off in range(1, group):
        peer = mine * group + lax.rem(place + off, group)
        pl.semaphore_signal(barrier, inc=1, device_id=(peer, h), device_id_type=MESH)
    pl.semaphore_wait(barrier, heads_here - 1 + group - 1)

    def pieces(head, slot):
        out = []
        for i in range(5):
            ref, at = (wq_ref, i) if i < 3 else (wt_ref, i - 3)
            start = pl.multiple_of(at * width + head * HD, HD)
            out.append((ref.at[:, pl.ds(start, HD)], w_ref.at[slot, :, pl.ds(i * HD, HD)]))
        out.append((ctx_ref, full_ref.at[slot]))
        return out

    def first(off, slot):
        head = lax.rem(mine + off, heads_here)
        return [
            pltpu.make_async_remote_copy(
                src_ref=src,
                dst_ref=dst,
                send_sem=send_sem.at[off, i],
                recv_sem=recv_sem.at[off, i],
                device_id=(head * group + place, h),
                device_id_type=MESH,
            )
            for i, (src, dst) in enumerate(pieces(head, slot))
        ]

    def second(off, piece, slot):
        peer = mine * group + lax.rem(place + off, group)
        return [
            pltpu.make_async_remote_copy(
                src_ref=ref.at[slot],
                dst_ref=ref.at[slot],
                send_sem=pass_send.at[off, piece, i],
                recv_sem=pass_recv.at[off, piece, i],
                device_id=(peer, h),
                device_id_type=MESH,
            )
            for i, ref in enumerate((w_ref, full_ref))
        ]

    for off in range(1, heads_here):
        for copy in first(off, s):
            copy.start()
    own = [
        pltpu.make_async_copy(src, dst, local_sem.at[i])
        for i, (src, dst) in enumerate(pieces(mine, s))
    ]
    for copy in own:
        copy.start()
    for copy in own:
        copy.wait()
    for piece in range(heads_here):
        slot = lax.rem(mine + heads_here - piece, heads_here) * group + place
        if piece > 0:
            for copy in first(piece, slot):
                copy.wait_recv()
        for off in range(1, group):
            for copy in second(off, piece, slot):
                copy.start()
    for off in range(1, heads_here):
        for copy in first(off, s):
            copy.wait_send()
    for piece in range(heads_here):
        from_group = lax.rem(mine + heads_here - piece, heads_here) * group
        for off in range(1, group):
            for copy in second(off, piece, from_group + place):
                copy.wait_send()
            for copy in second(off, piece, from_group + lax.rem(place + group - off, group)):
                copy.wait_recv()


def gather_weights(w_qkv, w_text, own_context):
    seq_n = lax.axis_size("seq")
    depth, _, head_width = w_qkv.shape
    heads_here = head_width // HD
    group = seq_n // heads_here
    text_count = own_context.shape[1]
    anywhere = pl.BlockSpec(memory_space=pl.ANY)
    sems = pltpu.SemaphoreType.DMA
    return pl.pallas_call(
        functools.partial(weights_kernel, heads_here, group),
        out_shape=(
            jax.ShapeDtypeStruct((seq_n, depth, 5 * HD), w_qkv.dtype),
            jax.ShapeDtypeStruct((seq_n, depth, text_count), own_context.dtype),
        ),
        in_specs=[anywhere] * 3,
        out_specs=(anywhere, anywhere),
        scratch_shapes=[
            sems((6,)),
            sems((heads_here, 6)),
            sems((heads_here, 6)),
            sems((group, heads_here, 2)),
            sems((group, heads_here, 2)),
        ],
        compiler_params=pltpu.CompilerParams(collective_id=2, has_side_effects=True),
    )(w_qkv.reshape(depth, 3 * head_width), w_text.reshape(depth, 2 * head_width), own_context)


def group_norm(features, gn_gain, gn_bias):
    frame_count, row_count, col_count, chan_count = features.shape
    per_group = chan_count // GN_GROUPS
    values = features.astype(jnp.float32)
    chan_sums = jnp.stack(
        [jnp.sum(values, axis=(0, 1, 2)), jnp.sum(values * values, axis=(0, 1, 2))]
    )
    sums = jnp.sum(chan_sums.reshape(2, GN_GROUPS, per_group), axis=2)
    block = jnp.pad(sums, ((0, 6), (0, 128 - GN_GROUPS)))
    sums = jnp.sum(share(block, 0), axis=0)[:2, :GN_GROUPS]
    cell_count = (
        frame_count * row_count * col_count * per_group * lax.axis_size("seq") * lax.axis_size("head")
    )
    mean = sums[0] / cell_count
    scale = lax.rsqrt(sums[1] / cell_count - mean * mean + eps_norm)
    mean = jnp.repeat(mean, per_group)
    scale = jnp.repeat(scale, per_group)
    normed = (values - mean) * scale
    return jax.nn.silu(normed * gn_gain + gn_bias).astype(jnp.bfloat16)


def join_rims(parts, block_dim, dim, unit):
    size = parts.shape[dim]
    blocks = parts.shape[block_dim]
    core = lax.slice_in_dim(parts, unit, size - unit, axis=dim)
    low = lax.slice_in_dim(parts, 0, unit, axis=dim)
    high = lax.slice_in_dim(parts, size - unit, size, axis=dim)
    low = lax.slice_in_dim(low, 1, blocks, axis=block_dim)
    high = lax.slice_in_dim(high, 0, blocks - 1, axis=block_dim)
    pad_low = [(0, 0)] * parts.ndim
    pad_low[block_dim] = (0, 1)
    pad_low[dim] = (size - 3 * unit, 0)
    pad_high = [(0, 0)] * parts.ndim
    pad_high[block_dim] = (1, 0)
    pad_high[dim] = (0, size - 3 * unit)
    return core + jnp.pad(low, pad_low) + jnp.pad(high, pad_high)


def all_patches(activated, conv_weight, conv_bias):
    seq_n, head_n = lax.axis_size("seq"), lax.axis_size("head")
    frame_count, row_count, col_count, _ = activated.shape
    chans = conv_weight.shape[3]
    padded = jnp.concatenate([activated[:1], activated[:1], activated], axis=0)
    shares = lax.conv_general_dilated(
        padded[None],
        conv_weight,
        (1, 1, 1),
        ((0, 0), (2, 2), (2, 2)),
        dimension_numbers=("NDHWC", "DHWOI", "NDHWC"),
        preferred_element_type=jnp.float32,
    )[0]
    flat = shares.reshape(-1, 128)
    parts = share(flat, 1)
    parts = parts.reshape(
        seq_n, head_n, frame_count, row_count + 2, (col_count + 2) * chans
    )
    parts = join_rims(join_rims(parts, 0, 3, 1), 1, 4, chans)
    latent = (parts + jnp.tile(conv_bias, col_count)).astype(jnp.bfloat16)
    blocks = latent.reshape(
        seq_n, head_n, frame_count, row_count // 2, 2, col_count // 2, 2 * chans
    )
    blocks = blocks.transpose(0, 1, 2, 3, 5, 4, 6)
    own = frame_count * (row_count // 2) * (col_count // 2)
    return blocks.reshape(seq_n * head_n * own, 4 * chans)


def modulate(patches, patch_weight, patch_bias, image_mod):
    hidden = jnp.dot(patches, patch_weight, preferred_element_type=jnp.float32) + patch_bias
    center = jnp.mean(hidden, axis=1, keepdims=True)
    offset = hidden - center
    spread = jnp.mean(offset * offset, axis=1, keepdims=True)
    normed = offset * lax.rsqrt(spread + eps_norm)
    return (normed * (1.0 + image_mod[1]) + image_mod[0]).astype(jnp.bfloat16)


def body(
    features,
    gn_gain,
    gn_bias,
    conv_weight,
    conv_bias,
    patch_weight,
    patch_bias,
    image_mod,
    w_qkv,
    text_ids,
    text_length,
    text_table,
    text_mod,
    w_text,
    w_out,
    out_bias,
):
    frame_count, row_count, col_count, _ = features.shape
    width_full = patch_weight.shape[1]
    seq_n, head_n = lax.axis_size("seq"), lax.axis_size("head")
    seq_i, head_i = lax.axis_index("seq"), lax.axis_index("head")
    depth, _, head_width = w_qkv.shape
    heads_here = head_width // HD
    group = seq_n // heads_here
    text_count = text_ids.shape[0]

    chosen = (
        lax.broadcasted_iota(jnp.int32, (text_table.shape[1], text_count), 0) == text_ids[None, :]
    ).astype(jnp.bfloat16)
    own_context = jnp.dot(text_table, chosen, preferred_element_type=jnp.float32).astype(
        jnp.bfloat16
    )
    weights, context = gather_weights(w_qkv, w_text, own_context)
    weights = weights.reshape(width_full, 5 * HD)
    context = context.reshape(width_full, text_count).astype(jnp.float32)
    mod = lax.all_gather(text_mod, "seq", axis=1, tiled=True)
    text_mean = jnp.sum(context, axis=0) / width_full
    text_square = jnp.sum(context * context, axis=0) / width_full
    text_scale = lax.rsqrt(text_square - text_mean * text_mean + eps_norm)
    text_normed = (context - text_mean) * text_scale * (1.0 + mod[1][:, None]) + mod[0][:, None]
    text_high = text_normed.astype(jnp.bfloat16)
    text_low = (text_normed - text_high.astype(jnp.float32)).astype(jnp.bfloat16)
    w_text_flat = weights[:, 3 * HD :]
    text_kv = sum(
        lax.dot_general(
            part, w_text_flat, (((0,), (0,)), ((), ())), preferred_element_type=jnp.float32
        )
        for part in (text_high, text_low)
    ).astype(jnp.bfloat16)

    activated = group_norm(features, gn_gain, gn_bias)
    patches = all_patches(activated, conv_weight, conv_bias)
    own = patches.shape[0] // (seq_n * head_n)
    part_rows = head_n * own // group
    my_part = seq_i % group
    chunk = min(CHUNK, patches.shape[0])

    def project(rows):
        modulated = modulate(rows, patch_weight, patch_bias, image_mod)
        qkv = jnp.dot(modulated, weights[:, : 3 * HD], preferred_element_type=jnp.float32)
        query, kv = qkv[:, :HD], qkv[:, HD:]
        query = lax.dynamic_index_in_dim(
            query.reshape(-1, group, part_rows, HD), my_part, axis=1, keepdims=False
        )
        return kv.astype(jnp.bfloat16), query.reshape(-1, HD).astype(jnp.bfloat16)

    if chunk == patches.shape[0]:
        image_kv, query = project(patches)
    else:
        image_kv, query = lax.map(project, patches.reshape(-1, chunk, patches.shape[1]))
        image_kv = image_kv.reshape(-1, 2 * HD)
        query = query.reshape(-1, HD)

    keys = jnp.concatenate([image_kv[:, :HD], text_kv[:, :HD]], axis=0)
    vals = jnp.concatenate([image_kv[:, HD:], text_kv[:, HD:]], axis=0)
    key_valid = (
        jnp.arange(keys.shape[0], dtype=jnp.int32) < image_kv.shape[0] + text_length[0]
    )
    scores = (
        lax.dot_general(query, keys, (((1,), (1,)), ((), ())), preferred_element_type=jnp.float32)
        / HD
    )
    scores = jnp.where(key_valid[None, :], scores, -1e30)
    probs = jnp.exp(scores - jnp.max(scores, axis=1, keepdims=True))
    totals = jnp.sum(probs, axis=1, keepdims=True)
    attended = (
        jnp.dot(probs.astype(jnp.bfloat16), vals, preferred_element_type=jnp.float32) / totals
    ).astype(jnp.bfloat16)

    attended = attended.reshape(seq_n, part_rows, HD)
    attended = lax.all_to_all(attended, "seq", split_axis=0, concat_axis=0, tiled=True)
    attended = attended.reshape(heads_here, group, part_rows, HD).transpose(1, 2, 0, 3)
    attended = attended.reshape(head_n * own, head_width)
    if head_n == 2:
        halves = attended.reshape(2, own, head_width)
        away = jnp.dot(
            lax.dynamic_index_in_dim(halves, 1 - head_i, 0, keepdims=False),
            w_out,
            preferred_element_type=jnp.float32,
        )
        here = jnp.dot(
            lax.dynamic_index_in_dim(halves, head_i, 0, keepdims=False),
            w_out,
            preferred_element_type=jnp.float32,
        )
        projected = here + lax.ppermute(away, "head", [(0, 1), (1, 0)]) + out_bias
    else:
        projected = (
            lax.psum_scatter(
                jnp.dot(attended, w_out, preferred_element_type=jnp.float32),
                "head",
                scatter_dimension=0,
                tiled=True,
            )
            + out_bias
        )
    own_patches = lax.dynamic_slice_in_dim(patches, (seq_i * head_n + head_i) * own, own, axis=0)
    hidden = jnp.dot(own_patches, patch_weight, preferred_element_type=jnp.float32) + patch_bias
    block_out = (hidden + image_mod[2] * projected).astype(jnp.bfloat16)
    return block_out.reshape(frame_count, row_count // 2, col_count // 2, width_full)


def solution(mesh):
    return jax.shard_map(
        body,
        mesh=mesh,
        in_specs=(
            P(None, "seq", "head", None),
            P(),
            P(),
            P(),
            P(),
            P(),
            P(),
            P(),
            P("seq", None, "head"),
            P(),
            P(),
            P("seq", None),
            P(None, "seq"),
            P("seq", None, "head"),
            P("head", None),
            P(),
        ),
        out_specs=P(None, "seq", "head", None),
        check_vma=False,
    )
```

```python
import functools

import jax
import jax.numpy as jnp
from jax import lax
from jax.experimental import pallas as pl
from jax.experimental.pallas import tpu as pltpu
from jax.sharding import PartitionSpec as P

HD = 128
GN_GROUPS = 32
CHUNK = 512

eps_norm = 1e-06


MESH = pl.DeviceIdType.MESH


def place_of(index, head_n):
    return (lax.div(index, head_n), lax.rem(index, head_n))


def greet_all(seq_n, head_n):
    count = seq_n * head_n
    me = lax.axis_index("seq") * head_n + lax.axis_index("head")
    barrier = pltpu.get_barrier_semaphore()

    def greet(off, carry):
        pl.semaphore_signal(
            barrier,
            inc=1,
            device_id=place_of(lax.rem(me + off, count), head_n),
            device_id_type=MESH,
        )
        return carry

    lax.fori_loop(1, count, greet, 0)
    pl.semaphore_wait(barrier, count - 1)


def start_share(seq_n, head_n, x_ref, out_ref, local_sem, send_sem, recv_sem):
    count = seq_n * head_n
    me = lax.axis_index("seq") * head_n + lax.axis_index("head")

    def copy(off, slot):
        return pltpu.make_async_remote_copy(
            src_ref=x_ref,
            dst_ref=out_ref.at[slot],
            send_sem=send_sem.at[off],
            recv_sem=recv_sem.at[off],
            device_id=place_of(lax.rem(me + off, count), head_n),
            device_id_type=MESH,
        )

    def send(off, carry):
        copy(off, me).start()
        return carry

    lax.fori_loop(1, count, send, 0)
    own = pltpu.make_async_copy(x_ref, out_ref.at[me], local_sem)
    own.start()

    def finish():
        own.wait()

        def wait(off, carry):
            copy(off, me).wait_send()
            copy(off, lax.rem(me + count - off, count)).wait_recv()
            return carry

        lax.fori_loop(1, count, wait, 0)

    return finish


def share_kernel(seq_n, head_n, x_ref, out_ref, local_sem, send_sem, recv_sem):
    greet_all(seq_n, head_n)
    start_share(seq_n, head_n, x_ref, out_ref, local_sem, send_sem, recv_sem)()


def swap_kernel(seq_n, x_ref, out_ref, local_sem, send_sem, recv_sem):
    me, h = lax.axis_index("seq"), lax.axis_index("head")
    barrier = pltpu.get_barrier_semaphore()

    def greet(off, carry):
        pl.semaphore_signal(
            barrier, inc=1, device_id=(lax.rem(me + off, seq_n), h), device_id_type=MESH
        )
        return carry

    lax.fori_loop(1, seq_n, greet, 0)
    pl.semaphore_wait(barrier, seq_n - 1)

    def copy(off, slot):
        peer = lax.rem(me + off, seq_n)
        return pltpu.make_async_remote_copy(
            src_ref=x_ref.at[peer],
            dst_ref=out_ref.at[slot],
            send_sem=send_sem.at[off],
            recv_sem=recv_sem.at[off],
            device_id=(peer, h),
            device_id_type=MESH,
        )

    def send(off, carry):
        copy(off, me).start()
        return carry

    lax.fori_loop(1, seq_n, send, 0)
    own = pltpu.make_async_copy(x_ref.at[me], out_ref.at[me], local_sem)
    own.start()
    own.wait()

    def wait(off, carry):
        copy(off, me).wait_send()
        copy(off, lax.rem(me + seq_n - off, seq_n)).wait_recv()
        return carry

    lax.fori_loop(1, seq_n, wait, 0)


def swap(x):
    seq_n = lax.axis_size("seq")
    return pl.pallas_call(
        functools.partial(swap_kernel, seq_n),
        out_shape=jax.ShapeDtypeStruct(x.shape, x.dtype),
        in_specs=[pl.BlockSpec(memory_space=pltpu.VMEM)],
        out_specs=pl.BlockSpec(memory_space=pltpu.VMEM),
        scratch_shapes=[
            pltpu.SemaphoreType.DMA,
            pltpu.SemaphoreType.DMA((seq_n,)),
            pltpu.SemaphoreType.DMA((seq_n,)),
        ],
        compiler_params=pltpu.CompilerParams(collective_id=1, has_side_effects=True),
    )(x)


def share(x, collective_id):
    seq_n, head_n = lax.axis_size("seq"), lax.axis_size("head")
    count = seq_n * head_n
    return pl.pallas_call(
        functools.partial(share_kernel, seq_n, head_n),
        out_shape=jax.ShapeDtypeStruct((count, *x.shape), x.dtype),
        in_specs=[pl.BlockSpec(memory_space=pltpu.VMEM)],
        out_specs=pl.BlockSpec(memory_space=pltpu.VMEM),
        scratch_shapes=[
            pltpu.SemaphoreType.DMA,
            pltpu.SemaphoreType.DMA((count,)),
            pltpu.SemaphoreType.DMA((count,)),
        ],
        compiler_params=pltpu.CompilerParams(collective_id=collective_id, has_side_effects=True),
    )(x)


def weights_kernel(
    heads_here,
    group,
    wq_ref,
    wt_ref,
    ctx_ref,
    x_ref,
    w_ref,
    full_ref,
    parts_ref,
    local_sem,
    send_sem,
    recv_sem,
    pass_send,
    pass_recv,
    share_local,
    share_send,
    share_recv,
):
    s, h = lax.axis_index("seq"), lax.axis_index("head")
    mine, place = lax.div(s, group), lax.rem(s, group)
    width = heads_here * HD
    greet_all(lax.axis_size("seq"), lax.axis_size("head"))
    finish_share = start_share(
        lax.axis_size("seq"), lax.axis_size("head"), x_ref, parts_ref, share_local, share_send, share_recv
    )

    def pieces(head, slot):
        out = []
        for i in range(5):
            ref, at = (wq_ref, i) if i < 3 else (wt_ref, i - 3)
            start = pl.multiple_of(at * width + head * HD, HD)
            out.append((ref.at[:, pl.ds(start, HD)], w_ref.at[slot, :, pl.ds(i * HD, HD)]))
        out.append((ctx_ref, full_ref.at[slot]))
        return out

    def first(off, slot):
        head = lax.rem(mine + off, heads_here)
        return [
            pltpu.make_async_remote_copy(
                src_ref=src,
                dst_ref=dst,
                send_sem=send_sem.at[off, i],
                recv_sem=recv_sem.at[off, i],
                device_id=(head * group + place, h),
                device_id_type=MESH,
            )
            for i, (src, dst) in enumerate(pieces(head, slot))
        ]

    def second(off, piece, slot):
        peer = mine * group + lax.rem(place + off, group)
        return [
            pltpu.make_async_remote_copy(
                src_ref=ref.at[slot],
                dst_ref=ref.at[slot],
                send_sem=pass_send.at[off, piece, i],
                recv_sem=pass_recv.at[off, piece, i],
                device_id=(peer, h),
                device_id_type=MESH,
            )
            for i, ref in enumerate((w_ref, full_ref))
        ]

    for off in range(1, heads_here):
        for copy in first(off, s):
            copy.start()
    own = [
        pltpu.make_async_copy(src, dst, local_sem.at[i])
        for i, (src, dst) in enumerate(pieces(mine, s))
    ]
    for copy in own:
        copy.start()
    for copy in own:
        copy.wait()
    for piece in range(heads_here):
        slot = lax.rem(mine + heads_here - piece, heads_here) * group + place
        if piece > 0:
            for copy in first(piece, slot):
                copy.wait_recv()
        for off in range(1, group):
            for copy in second(off, piece, slot):
                copy.start()
    for off in range(1, heads_here):
        for copy in first(off, s):
            copy.wait_send()
    for piece in range(heads_here):
        from_group = lax.rem(mine + heads_here - piece, heads_here) * group
        for off in range(1, group):
            for copy in second(off, piece, from_group + place):
                copy.wait_send()
            for copy in second(off, piece, from_group + lax.rem(place + group - off, group)):
                copy.wait_recv()
    finish_share()


def gather_weights(w_qkv, w_text, own_context, shares):
    seq_n = lax.axis_size("seq")
    depth, _, head_width = w_qkv.shape
    heads_here = head_width // HD
    group = seq_n // heads_here
    count = seq_n * lax.axis_size("head")
    text_count = own_context.shape[1]
    anywhere = pl.BlockSpec(memory_space=pl.ANY)
    sems = pltpu.SemaphoreType.DMA
    return pl.pallas_call(
        functools.partial(weights_kernel, heads_here, group),
        out_shape=(
            jax.ShapeDtypeStruct((seq_n, depth, 5 * HD), w_qkv.dtype),
            jax.ShapeDtypeStruct((seq_n, depth, text_count), own_context.dtype),
            jax.ShapeDtypeStruct((count, *shares.shape), shares.dtype),
        ),
        in_specs=[anywhere] * 3 + [pl.BlockSpec(memory_space=pltpu.VMEM)],
        out_specs=(anywhere, anywhere, pl.BlockSpec(memory_space=pltpu.VMEM)),
        scratch_shapes=[
            sems((6,)),
            sems((heads_here, 6)),
            sems((heads_here, 6)),
            sems((group, heads_here, 2)),
            sems((group, heads_here, 2)),
            sems,
            sems((count,)),
            sems((count,)),
        ],
        compiler_params=pltpu.CompilerParams(collective_id=2, has_side_effects=True),
    )(w_qkv.reshape(depth, 3 * head_width), w_text.reshape(depth, 2 * head_width), own_context, shares)


def group_norm(features, gn_gain, gn_bias, text_mod):
    frame_count, row_count, col_count, chan_count = features.shape
    per_group = chan_count // GN_GROUPS
    values = features.astype(jnp.float32)
    chan_sums = jnp.stack(
        [jnp.sum(values, axis=(0, 1, 2)), jnp.sum(values * values, axis=(0, 1, 2))]
    )
    sums = jnp.sum(chan_sums.reshape(2, GN_GROUPS, per_group), axis=2)
    seq_n, head_n = lax.axis_size("seq"), lax.axis_size("head")
    depth = text_mod.shape[1]
    lines = -(-depth // 128)
    mod = jnp.pad(text_mod, ((0, 0), (0, lines * 128 - depth))).reshape(2 * lines, 128)
    block = jnp.concatenate([jnp.pad(sums, ((0, 0), (0, 128 - GN_GROUPS))), mod], axis=0)
    block = jnp.pad(block, ((0, -block.shape[0] % 8), (0, 0)))
    shared = share(block, 0)
    sums = jnp.sum(shared[:, :2, :GN_GROUPS], axis=0)
    mod = shared.reshape(seq_n, head_n, -1, 128)[:, 0, 2 : 2 + 2 * lines]
    mod = mod.reshape(seq_n, 2, lines * 128)[:, :, :depth]
    mod = mod.transpose(1, 0, 2).reshape(2, seq_n * depth)
    cell_count = (
        frame_count * row_count * col_count * per_group * lax.axis_size("seq") * lax.axis_size("head")
    )
    mean = sums[0] / cell_count
    scale = lax.rsqrt(sums[1] / cell_count - mean * mean + eps_norm)
    mean = jnp.repeat(mean, per_group)
    scale = jnp.repeat(scale, per_group)
    normed = (values - mean) * scale
    return jax.nn.silu(normed * gn_gain + gn_bias).astype(jnp.bfloat16), mod


def join_rims(parts, block_dim, dim, unit):
    size = parts.shape[dim]
    blocks = parts.shape[block_dim]
    core = lax.slice_in_dim(parts, unit, size - unit, axis=dim)
    low = lax.slice_in_dim(parts, 0, unit, axis=dim)
    high = lax.slice_in_dim(parts, size - unit, size, axis=dim)
    low = lax.slice_in_dim(low, 1, blocks, axis=block_dim)
    high = lax.slice_in_dim(high, 0, blocks - 1, axis=block_dim)
    pad_low = [(0, 0)] * parts.ndim
    pad_low[block_dim] = (0, 1)
    pad_low[dim] = (size - 3 * unit, 0)
    pad_high = [(0, 0)] * parts.ndim
    pad_high[block_dim] = (1, 0)
    pad_high[dim] = (0, size - 3 * unit)
    return core + jnp.pad(low, pad_low) + jnp.pad(high, pad_high)


def conv_shares(activated, conv_weight):
    padded = jnp.concatenate([activated[:1], activated[:1], activated], axis=0)
    shares = lax.conv_general_dilated(
        padded[None],
        conv_weight,
        (1, 1, 1),
        ((0, 0), (2, 2), (2, 2)),
        dimension_numbers=("NDHWC", "DHWOI", "NDHWC"),
        preferred_element_type=jnp.float32,
    )[0]
    return shares.reshape(-1, 128)


def all_patches(parts, frame_count, row_count, col_count, conv_bias):
    seq_n, head_n = lax.axis_size("seq"), lax.axis_size("head")
    chans = conv_bias.shape[0]
    parts = parts.reshape(
        seq_n, head_n, frame_count, row_count + 2, (col_count + 2) * chans
    )
    parts = join_rims(join_rims(parts, 0, 3, 1), 1, 4, chans)
    latent = (parts + jnp.tile(conv_bias, col_count)).astype(jnp.bfloat16)
    blocks = latent.reshape(
        seq_n, head_n, frame_count, row_count // 2, 2, col_count // 2, 2 * chans
    )
    blocks = blocks.transpose(0, 1, 2, 3, 5, 4, 6)
    own = frame_count * (row_count // 2) * (col_count // 2)
    return blocks.reshape(seq_n * head_n * own, 4 * chans)


def modulate(patches, patch_weight, patch_bias, image_mod):
    hidden = jnp.dot(patches, patch_weight, preferred_element_type=jnp.float32) + patch_bias
    center = jnp.mean(hidden, axis=1, keepdims=True)
    offset = hidden - center
    spread = jnp.mean(offset * offset, axis=1, keepdims=True)
    normed = offset * lax.rsqrt(spread + eps_norm)
    return (normed * (1.0 + image_mod[1]) + image_mod[0]).astype(jnp.bfloat16)


def body(
    features,
    gn_gain,
    gn_bias,
    conv_weight,
    conv_bias,
    patch_weight,
    patch_bias,
    image_mod,
    w_qkv,
    text_ids,
    text_length,
    text_table,
    text_mod,
    w_text,
    w_out,
    out_bias,
):
    frame_count, row_count, col_count, _ = features.shape
    width_full = patch_weight.shape[1]
    seq_n, head_n = lax.axis_size("seq"), lax.axis_size("head")
    seq_i, head_i = lax.axis_index("seq"), lax.axis_index("head")
    depth, _, head_width = w_qkv.shape
    heads_here = head_width // HD
    group = seq_n // heads_here
    text_count = text_ids.shape[0]

    chosen = (
        lax.broadcasted_iota(jnp.int32, (text_table.shape[1], text_count), 0) == text_ids[None, :]
    ).astype(jnp.bfloat16)
    own_context = jnp.dot(text_table, chosen, preferred_element_type=jnp.float32).astype(
        jnp.bfloat16
    )
    activated, mod = group_norm(features, gn_gain, gn_bias, text_mod)
    shares = conv_shares(activated, conv_weight)
    weights, context, parts = gather_weights(w_qkv, w_text, own_context, shares)
    weights = weights.reshape(width_full, 5 * HD)
    context = context.reshape(width_full, text_count).astype(jnp.float32)
    text_mean = jnp.sum(context, axis=0) / width_full
    text_square = jnp.sum(context * context, axis=0) / width_full
    text_scale = lax.rsqrt(text_square - text_mean * text_mean + eps_norm)
    text_normed = (context - text_mean) * text_scale * (1.0 + mod[1][:, None]) + mod[0][:, None]
    text_high = text_normed.astype(jnp.bfloat16)
    text_low = (text_normed - text_high.astype(jnp.float32)).astype(jnp.bfloat16)
    w_text_flat = weights[:, 3 * HD :]
    text_kv = sum(
        lax.dot_general(
            part, w_text_flat, (((0,), (0,)), ((), ())), preferred_element_type=jnp.float32
        )
        for part in (text_high, text_low)
    ).astype(jnp.bfloat16)

    patches = all_patches(parts, frame_count, row_count, col_count, conv_bias)
    own = patches.shape[0] // (seq_n * head_n)
    part_rows = head_n * own // group
    my_part = seq_i % group
    chunk = min(CHUNK, patches.shape[0])

    def project(rows):
        modulated = modulate(rows, patch_weight, patch_bias, image_mod)
        qkv = jnp.dot(modulated, weights[:, : 3 * HD], preferred_element_type=jnp.float32)
        query, kv = qkv[:, :HD], qkv[:, HD:]
        query = lax.dynamic_index_in_dim(
            query.reshape(-1, group, part_rows, HD), my_part, axis=1, keepdims=False
        )
        return kv.astype(jnp.bfloat16), query.reshape(-1, HD).astype(jnp.bfloat16)

    if chunk == patches.shape[0]:
        image_kv, query = project(patches)
    else:
        image_kv, query = lax.map(project, patches.reshape(-1, chunk, patches.shape[1]))
        image_kv = image_kv.reshape(-1, 2 * HD)
        query = query.reshape(-1, HD)

    keys = jnp.concatenate([image_kv[:, :HD], text_kv[:, :HD]], axis=0)
    vals = jnp.concatenate([image_kv[:, HD:], text_kv[:, HD:]], axis=0)
    key_valid = (
        jnp.arange(keys.shape[0], dtype=jnp.int32) < image_kv.shape[0] + text_length[0]
    )
    scores = (
        lax.dot_general(query, keys, (((1,), (1,)), ((), ())), preferred_element_type=jnp.float32)
        / HD
    )
    scores = jnp.where(key_valid[None, :], scores, -1e30)
    probs = jnp.exp(scores - jnp.max(scores, axis=1, keepdims=True))
    totals = jnp.sum(probs, axis=1, keepdims=True)
    attended = (
        jnp.dot(probs.astype(jnp.bfloat16), vals, preferred_element_type=jnp.float32) / totals
    ).astype(jnp.bfloat16)

    attended = attended.reshape(seq_n, part_rows, HD)
    attended = swap(attended)
    attended = attended.reshape(heads_here, group, part_rows, HD).transpose(1, 2, 0, 3)
    attended = attended.reshape(head_n * own, head_width)
    if head_n == 2:
        halves = jnp.dot(attended, w_out, preferred_element_type=jnp.float32)
        halves = halves.reshape(2, own, width_full)
        away = lax.dynamic_index_in_dim(halves, 1 - head_i, 0, keepdims=False)
        here = lax.dynamic_index_in_dim(halves, head_i, 0, keepdims=False)
        projected = here + lax.ppermute(away, "head", [(0, 1), (1, 0)]) + out_bias
    else:
        projected = (
            lax.psum_scatter(
                jnp.dot(attended, w_out, preferred_element_type=jnp.float32),
                "head",
                scatter_dimension=0,
                tiled=True,
            )
            + out_bias
        )
    own_patches = lax.dynamic_slice_in_dim(patches, (seq_i * head_n + head_i) * own, own, axis=0)
    hidden = jnp.dot(own_patches, patch_weight, preferred_element_type=jnp.float32) + patch_bias
    block_out = (hidden + image_mod[2] * projected).astype(jnp.bfloat16)
    return block_out.reshape(frame_count, row_count // 2, col_count // 2, width_full)


def solution(mesh):
    return jax.shard_map(
        body,
        mesh=mesh,
        in_specs=(
            P(None, "seq", "head", None),
            P(),
            P(),
            P(),
            P(),
            P(),
            P(),
            P(),
            P("seq", None, "head"),
            P(),
            P(),
            P("seq", None),
            P(None, "seq"),
            P("seq", None, "head"),
            P("head", None),
            P(),
        ),
        out_specs=P(None, "seq", "head", None),
        check_vma=False,
    )
```

```python
import functools

import jax
import jax.numpy as jnp
from jax import lax
from jax.experimental import pallas as pl
from jax.experimental.pallas import tpu as pltpu
from jax.sharding import PartitionSpec as P

HD = 128
GN_GROUPS = 32
CHUNK = 512

eps_norm = 1e-06


MESH = pl.DeviceIdType.MESH


def place_of(index, head_n):
    return (lax.div(index, head_n), lax.rem(index, head_n))


def greet_all(seq_n, head_n):
    count = seq_n * head_n
    me = lax.axis_index("seq") * head_n + lax.axis_index("head")
    barrier = pltpu.get_barrier_semaphore()

    def greet(off, carry):
        pl.semaphore_signal(
            barrier,
            inc=1,
            device_id=place_of(lax.rem(me + off, count), head_n),
            device_id_type=MESH,
        )
        return carry

    lax.fori_loop(1, count, greet, 0)
    pl.semaphore_wait(barrier, count - 1)


def start_share(seq_n, head_n, x_ref, out_ref, local_sem, send_sem, recv_sem):
    count = seq_n * head_n
    me = lax.axis_index("seq") * head_n + lax.axis_index("head")

    def copy(off, slot):
        return pltpu.make_async_remote_copy(
            src_ref=x_ref,
            dst_ref=out_ref.at[slot],
            send_sem=send_sem.at[off],
            recv_sem=recv_sem.at[off],
            device_id=place_of(lax.rem(me + off, count), head_n),
            device_id_type=MESH,
        )

    def send(off, carry):
        copy(off, me).start()
        return carry

    lax.fori_loop(1, count, send, 0)
    own = pltpu.make_async_copy(x_ref, out_ref.at[me], local_sem)
    own.start()

    def finish():
        own.wait()

        def wait(off, carry):
            copy(off, me).wait_send()
            copy(off, lax.rem(me + count - off, count)).wait_recv()
            return carry

        lax.fori_loop(1, count, wait, 0)

    return finish


def share_kernel(seq_n, head_n, x_ref, out_ref, local_sem, send_sem, recv_sem):
    greet_all(seq_n, head_n)
    start_share(seq_n, head_n, x_ref, out_ref, local_sem, send_sem, recv_sem)()


def swap_kernel(seq_n, x_ref, out_ref, local_sem, send_sem, recv_sem):
    me, h = lax.axis_index("seq"), lax.axis_index("head")
    barrier = pltpu.get_barrier_semaphore()

    def greet(off, carry):
        pl.semaphore_signal(
            barrier, inc=1, device_id=(lax.rem(me + off, seq_n), h), device_id_type=MESH
        )
        return carry

    lax.fori_loop(1, seq_n, greet, 0)
    pl.semaphore_wait(barrier, seq_n - 1)

    def copy(off, slot):
        peer = lax.rem(me + off, seq_n)
        return pltpu.make_async_remote_copy(
            src_ref=x_ref.at[peer],
            dst_ref=out_ref.at[slot],
            send_sem=send_sem.at[off],
            recv_sem=recv_sem.at[off],
            device_id=(peer, h),
            device_id_type=MESH,
        )

    def send(off, carry):
        copy(off, me).start()
        return carry

    lax.fori_loop(1, seq_n, send, 0)
    own = pltpu.make_async_copy(x_ref.at[me], out_ref.at[me], local_sem)
    own.start()
    own.wait()

    def wait(off, carry):
        copy(off, me).wait_send()
        copy(off, lax.rem(me + seq_n - off, seq_n)).wait_recv()
        return carry

    lax.fori_loop(1, seq_n, wait, 0)


def swap(x):
    seq_n = lax.axis_size("seq")
    return pl.pallas_call(
        functools.partial(swap_kernel, seq_n),
        out_shape=jax.ShapeDtypeStruct(x.shape, x.dtype),
        in_specs=[pl.BlockSpec(memory_space=pltpu.VMEM)],
        out_specs=pl.BlockSpec(memory_space=pltpu.VMEM),
        scratch_shapes=[
            pltpu.SemaphoreType.DMA,
            pltpu.SemaphoreType.DMA((seq_n,)),
            pltpu.SemaphoreType.DMA((seq_n,)),
        ],
        compiler_params=pltpu.CompilerParams(collective_id=1, has_side_effects=True),
    )(x)


def share(x, collective_id):
    seq_n, head_n = lax.axis_size("seq"), lax.axis_size("head")
    count = seq_n * head_n
    return pl.pallas_call(
        functools.partial(share_kernel, seq_n, head_n),
        out_shape=jax.ShapeDtypeStruct((count, *x.shape), x.dtype),
        in_specs=[pl.BlockSpec(memory_space=pltpu.VMEM)],
        out_specs=pl.BlockSpec(memory_space=pltpu.VMEM),
        scratch_shapes=[
            pltpu.SemaphoreType.DMA,
            pltpu.SemaphoreType.DMA((count,)),
            pltpu.SemaphoreType.DMA((count,)),
        ],
        compiler_params=pltpu.CompilerParams(collective_id=collective_id, has_side_effects=True),
    )(x)


def weights_kernel(
    heads_here,
    group,
    halves,
    wq_ref,
    wt_ref,
    ctx_ref,
    x_ref,
    w_ref,
    full_ref,
    parts_ref,
    local_sem,
    send_sem,
    recv_sem,
    pass_send,
    pass_recv,
    over_send,
    over_recv,
    share_local,
    share_send,
    share_recv,
):
    s, h = lax.axis_index("seq"), lax.axis_index("head")
    mine, place = lax.div(s, group), lax.rem(s, group)
    width = heads_here * HD
    half = h if halves == 2 else 0
    greet_all(lax.axis_size("seq"), lax.axis_size("head"))
    finish_share = start_share(
        lax.axis_size("seq"), lax.axis_size("head"), x_ref, parts_ref, share_local, share_send, share_recv
    )

    def pieces(head, slot):
        out = [(ctx_ref, full_ref.at[half, slot])]
        for i in range(5):
            ref, at = (wq_ref, i) if i < 3 else (wt_ref, i - 3)
            start = pl.multiple_of(at * width + head * HD, HD)
            out.append((ref.at[:, pl.ds(start, HD)], w_ref.at[slot, :, pl.ds(i * HD, HD)]))
        return out

    def first(off, slot):
        head = lax.rem(mine + off, heads_here)
        return [
            pltpu.make_async_remote_copy(
                src_ref=src,
                dst_ref=dst,
                send_sem=send_sem.at[off, i],
                recv_sem=recv_sem.at[off, i],
                device_id=(head * group + place, h),
                device_id_type=MESH,
            )
            for i, (src, dst) in enumerate(pieces(head, slot))
        ]

    def second(off, piece, slot):
        peer = mine * group + lax.rem(place + off, group)
        return [
            pltpu.make_async_remote_copy(
                src_ref=ref,
                dst_ref=ref,
                send_sem=pass_send.at[off, piece, i],
                recv_sem=pass_recv.at[off, piece, i],
                device_id=(peer, h),
                device_id_type=MESH,
            )
            for i, ref in enumerate((w_ref.at[slot], full_ref.at[half, slot]))
        ]

    def over(off, piece, side, slot):
        peer = mine * group + lax.rem(place + off, group)
        return pltpu.make_async_remote_copy(
            src_ref=full_ref.at[side, slot],
            dst_ref=full_ref.at[side, slot],
            send_sem=over_send.at[off, piece],
            recv_sem=over_recv.at[off, piece],
            device_id=(peer, 1 - h),
            device_id_type=MESH,
        )

    for off in range(1, heads_here):
        for copy in first(off, s):
            copy.start()
    own = [
        pltpu.make_async_copy(src, dst, local_sem.at[i])
        for i, (src, dst) in enumerate(pieces(mine, s))
    ]
    for copy in own:
        copy.start()
    for copy in own:
        copy.wait()
    for piece in range(heads_here):
        slot = lax.rem(mine + heads_here - piece, heads_here) * group + place
        if piece > 0:
            arriving = first(piece, slot)
            arriving[0].wait_recv()
        if halves == 2:
            for off in range(group):
                over(off, piece, h, slot).start()
        if piece > 0:
            for copy in arriving[1:]:
                copy.wait_recv()
        for off in range(1, group):
            for copy in second(off, piece, slot):
                copy.start()
    for off in range(1, heads_here):
        for copy in first(off, s):
            copy.wait_send()
    for piece in range(heads_here):
        from_group = lax.rem(mine + heads_here - piece, heads_here) * group
        for off in range(1, group):
            for copy in second(off, piece, from_group + place):
                copy.wait_send()
            for copy in second(off, piece, from_group + lax.rem(place + group - off, group)):
                copy.wait_recv()
        if halves == 2:
            for off in range(group):
                over(off, piece, h, from_group + place).wait_send()
                there = from_group + lax.rem(place + group - off, group)
                over(off, piece, 1 - h, there).wait_recv()
    finish_share()


def gather_weights(w_qkv, w_text, own_context, shares, halves):
    seq_n = lax.axis_size("seq")
    depth, _, head_width = w_qkv.shape
    heads_here = head_width // HD
    group = seq_n // heads_here
    count = seq_n * lax.axis_size("head")
    text_count = own_context.shape[1]
    anywhere = pl.BlockSpec(memory_space=pl.ANY)
    sems = pltpu.SemaphoreType.DMA
    return pl.pallas_call(
        functools.partial(weights_kernel, heads_here, group, halves),
        out_shape=(
            jax.ShapeDtypeStruct((seq_n, depth, 5 * HD), w_qkv.dtype),
            jax.ShapeDtypeStruct((halves, seq_n, depth, text_count), own_context.dtype),
            jax.ShapeDtypeStruct((count, *shares.shape), shares.dtype),
        ),
        in_specs=[anywhere] * 3 + [pl.BlockSpec(memory_space=pltpu.VMEM)],
        out_specs=(anywhere, anywhere, pl.BlockSpec(memory_space=pltpu.VMEM)),
        scratch_shapes=[
            sems((6,)),
            sems((heads_here, 6)),
            sems((heads_here, 6)),
            sems((group, heads_here, 2)),
            sems((group, heads_here, 2)),
            sems((group, heads_here)),
            sems((group, heads_here)),
            sems,
            sems((count,)),
            sems((count,)),
        ],
        compiler_params=pltpu.CompilerParams(collective_id=2, has_side_effects=True),
    )(w_qkv.reshape(depth, 3 * head_width), w_text.reshape(depth, 2 * head_width), own_context, shares)


def group_norm(features, gn_gain, gn_bias, text_mod):
    frame_count, row_count, col_count, chan_count = features.shape
    per_group = chan_count // GN_GROUPS
    values = features.astype(jnp.float32)
    chan_sums = jnp.stack(
        [jnp.sum(values, axis=(0, 1, 2)), jnp.sum(values * values, axis=(0, 1, 2))]
    )
    sums = jnp.sum(chan_sums.reshape(2, GN_GROUPS, per_group), axis=2)
    seq_n, head_n = lax.axis_size("seq"), lax.axis_size("head")
    depth = text_mod.shape[1]
    lines = -(-depth // 128)
    mod = jnp.pad(text_mod, ((0, 0), (0, lines * 128 - depth))).reshape(2 * lines, 128)
    block = jnp.concatenate([jnp.pad(sums, ((0, 0), (0, 128 - GN_GROUPS))), mod], axis=0)
    block = jnp.pad(block, ((0, -block.shape[0] % 8), (0, 0)))
    shared = share(block, 0)
    sums = jnp.sum(shared[:, :2, :GN_GROUPS], axis=0)
    mod = shared.reshape(seq_n, head_n, -1, 128)[:, 0, 2 : 2 + 2 * lines]
    mod = mod.reshape(seq_n, 2, lines * 128)[:, :, :depth]
    mod = mod.transpose(1, 0, 2).reshape(2, seq_n * depth)
    cell_count = (
        frame_count * row_count * col_count * per_group * lax.axis_size("seq") * lax.axis_size("head")
    )
    mean = sums[0] / cell_count
    scale = lax.rsqrt(sums[1] / cell_count - mean * mean + eps_norm)
    mean = jnp.repeat(mean, per_group)
    scale = jnp.repeat(scale, per_group)
    normed = (values - mean) * scale
    return jax.nn.silu(normed * gn_gain + gn_bias).astype(jnp.bfloat16), mod


def join_rims(parts, block_dim, dim, unit):
    size = parts.shape[dim]
    blocks = parts.shape[block_dim]
    core = lax.slice_in_dim(parts, unit, size - unit, axis=dim)
    low = lax.slice_in_dim(parts, 0, unit, axis=dim)
    high = lax.slice_in_dim(parts, size - unit, size, axis=dim)
    low = lax.slice_in_dim(low, 1, blocks, axis=block_dim)
    high = lax.slice_in_dim(high, 0, blocks - 1, axis=block_dim)
    pad_low = [(0, 0)] * parts.ndim
    pad_low[block_dim] = (0, 1)
    pad_low[dim] = (size - 3 * unit, 0)
    pad_high = [(0, 0)] * parts.ndim
    pad_high[block_dim] = (1, 0)
    pad_high[dim] = (0, size - 3 * unit)
    return core + jnp.pad(low, pad_low) + jnp.pad(high, pad_high)


def conv_shares(activated, conv_weight):
    padded = jnp.concatenate([activated[:1], activated[:1], activated], axis=0)
    shares = lax.conv_general_dilated(
        padded[None],
        conv_weight,
        (1, 1, 1),
        ((0, 0), (2, 2), (2, 2)),
        dimension_numbers=("NDHWC", "DHWOI", "NDHWC"),
        preferred_element_type=jnp.float32,
    )[0]
    return shares.reshape(-1, 128)


def all_patches(parts, frame_count, row_count, col_count, conv_bias):
    seq_n, head_n = lax.axis_size("seq"), lax.axis_size("head")
    chans = conv_bias.shape[0]
    parts = parts.reshape(
        seq_n, head_n, frame_count, row_count + 2, (col_count + 2) * chans
    )
    parts = join_rims(join_rims(parts, 0, 3, 1), 1, 4, chans)
    latent = (parts + jnp.tile(conv_bias, col_count)).astype(jnp.bfloat16)
    blocks = latent.reshape(
        seq_n, head_n, frame_count, row_count // 2, 2, col_count // 2, 2 * chans
    )
    blocks = blocks.transpose(0, 1, 2, 3, 5, 4, 6)
    own = frame_count * (row_count // 2) * (col_count // 2)
    return blocks.reshape(seq_n * head_n * own, 4 * chans)


def modulate(patches, patch_weight, patch_bias, image_mod):
    hidden = jnp.dot(patches, patch_weight, preferred_element_type=jnp.float32) + patch_bias
    center = jnp.mean(hidden, axis=1, keepdims=True)
    offset = hidden - center
    spread = jnp.mean(offset * offset, axis=1, keepdims=True)
    normed = offset * lax.rsqrt(spread + eps_norm)
    return (normed * (1.0 + image_mod[1]) + image_mod[0]).astype(jnp.bfloat16)


def body(
    features,
    gn_gain,
    gn_bias,
    conv_weight,
    conv_bias,
    patch_weight,
    patch_bias,
    image_mod,
    w_qkv,
    text_ids,
    text_length,
    text_table,
    text_mod,
    w_text,
    w_out,
    out_bias,
):
    frame_count, row_count, col_count, _ = features.shape
    width_full = patch_weight.shape[1]
    seq_n, head_n = lax.axis_size("seq"), lax.axis_size("head")
    seq_i, head_i = lax.axis_index("seq"), lax.axis_index("head")
    depth, _, head_width = w_qkv.shape
    heads_here = head_width // HD
    group = seq_n // heads_here
    text_count = text_ids.shape[0]

    halves = 2 if head_n == 2 else 1
    count_here = text_count // halves
    ids_here = text_ids
    if halves == 2:
        ids_here = lax.dynamic_slice_in_dim(text_ids, head_i * count_here, count_here)
    chosen = (
        lax.broadcasted_iota(jnp.int32, (text_table.shape[1], count_here), 0) == ids_here[None, :]
    ).astype(jnp.bfloat16)
    own_context = jnp.dot(text_table, chosen, preferred_element_type=jnp.float32).astype(
        jnp.bfloat16
    )
    activated, mod = group_norm(features, gn_gain, gn_bias, text_mod)
    shares = conv_shares(activated, conv_weight)
    weights, context, parts = gather_weights(w_qkv, w_text, own_context, shares, halves)
    weights = weights.reshape(width_full, 5 * HD)
    context = context.reshape(halves, width_full, count_here).astype(jnp.float32)
    text_mean = jnp.sum(context, axis=1, keepdims=True) / width_full
    text_square = jnp.sum(context * context, axis=1, keepdims=True) / width_full
    text_scale = lax.rsqrt(text_square - text_mean * text_mean + eps_norm)
    text_normed = (context - text_mean) * text_scale * (1.0 + mod[1][:, None]) + mod[0][:, None]
    text_high = text_normed.astype(jnp.bfloat16)
    text_low = (text_normed - text_high.astype(jnp.float32)).astype(jnp.bfloat16)
    w_text_flat = weights[:, 3 * HD :]
    text_kv = sum(
        lax.dot_general(
            part, w_text_flat, (((1,), (0,)), ((), ())), preferred_element_type=jnp.float32
        )
        for part in (text_high, text_low)
    ).astype(jnp.bfloat16).reshape(text_count, 2 * HD)

    patches = all_patches(parts, frame_count, row_count, col_count, conv_bias)
    own = patches.shape[0] // (seq_n * head_n)
    part_rows = head_n * own // group
    my_part = seq_i % group
    chunk = min(CHUNK, patches.shape[0])

    def project(rows):
        modulated = modulate(rows, patch_weight, patch_bias, image_mod)
        qkv = jnp.dot(modulated, weights[:, : 3 * HD], preferred_element_type=jnp.float32)
        query, kv = qkv[:, :HD], qkv[:, HD:]
        query = lax.dynamic_index_in_dim(
            query.reshape(-1, group, part_rows, HD), my_part, axis=1, keepdims=False
        )
        return kv.astype(jnp.bfloat16), query.reshape(-1, HD).astype(jnp.bfloat16)

    if chunk == patches.shape[0]:
        image_kv, query = project(patches)
    else:
        image_kv, query = lax.map(project, patches.reshape(-1, chunk, patches.shape[1]))
        image_kv = image_kv.reshape(-1, 2 * HD)
        query = query.reshape(-1, HD)

    keys = jnp.concatenate([image_kv[:, :HD], text_kv[:, :HD]], axis=0)
    vals = jnp.concatenate([image_kv[:, HD:], text_kv[:, HD:]], axis=0)
    key_valid = (
        jnp.arange(keys.shape[0], dtype=jnp.int32) < image_kv.shape[0] + text_length[0]
    )
    scores = (
        lax.dot_general(query, keys, (((1,), (1,)), ((), ())), preferred_element_type=jnp.float32)
        / HD
    )
    scores = jnp.where(key_valid[None, :], scores, -1e30)
    probs = jnp.exp(scores - jnp.max(scores, axis=1, keepdims=True))
    totals = jnp.sum(probs, axis=1, keepdims=True)
    attended = (
        jnp.dot(probs.astype(jnp.bfloat16), vals, preferred_element_type=jnp.float32) / totals
    ).astype(jnp.bfloat16)

    attended = attended.reshape(seq_n, part_rows, HD)
    attended = swap(attended)
    attended = attended.reshape(heads_here, group, part_rows, HD).transpose(1, 2, 0, 3)
    attended = attended.reshape(head_n * own, head_width)
    if head_n == 2:
        halves = jnp.dot(attended, w_out, preferred_element_type=jnp.float32)
        halves = halves.reshape(2, own, width_full)
        away = lax.dynamic_index_in_dim(halves, 1 - head_i, 0, keepdims=False)
        here = lax.dynamic_index_in_dim(halves, head_i, 0, keepdims=False)
        projected = here + lax.ppermute(away, "head", [(0, 1), (1, 0)]) + out_bias
    else:
        projected = (
            lax.psum_scatter(
                jnp.dot(attended, w_out, preferred_element_type=jnp.float32),
                "head",
                scatter_dimension=0,
                tiled=True,
            )
            + out_bias
        )
    own_patches = lax.dynamic_slice_in_dim(patches, (seq_i * head_n + head_i) * own, own, axis=0)
    hidden = jnp.dot(own_patches, patch_weight, preferred_element_type=jnp.float32) + patch_bias
    block_out = (hidden + image_mod[2] * projected).astype(jnp.bfloat16)
    return block_out.reshape(frame_count, row_count // 2, col_count // 2, width_full)


def solution(mesh):
    return jax.shard_map(
        body,
        mesh=mesh,
        in_specs=(
            P(None, "seq", "head", None),
            P(),
            P(),
            P(),
            P(),
            P(),
            P(),
            P(),
            P("seq", None, "head"),
            P(),
            P(),
            P("seq", None),
            P(None, "seq"),
            P("seq", None, "head"),
            P("head", None),
            P(),
        ),
        out_specs=P(None, "seq", "head", None),
        check_vma=False,
    )
```
